128 devices in a mesh: band: 8 (over x, core), col: 16 (over y, z).
Axes of the slice: x: 4, y: 4, z: 4, core: 2. Of those that a mesh axis runs over, the one named last changes fastest.
Arguments:
- series: float32 [16, 32768], P(None, ('band', 'col')), may hold values from -6 to 6
- tail: float32 [16, 255], replicated, may hold values from -6 to 6
Outputs:
- profile: float32 [16, 32768], P(None, ('band', 'col'))
The draws below stay inside these ranges and needn't reach their ends.
All inputs are finite; a program needn't handle non-finite values.
Results may differ from the reference program's by a relative error of at most 0.0003.
Values may be sent and summed in bfloat16 or wider, within the bound.
No kernel may reach another device: no remote copies, remote signals or barrier semaphores. Data moves between devices by JAX's collectives and lax.ppermute only.
A program may use at most 64 MiB of HBM per device.

```python
import jax
import jax.numpy as jnp
from jax import lax

M = 256
CH = 16
TB = 256
KD = 4
EXCL = 64
NSUB = 32768
N_BAND = 8
N_COL = 16


def steps_of(own_key, shape, cuts, least, high):
    def one(axis_at, blocks):
        heights = jax.random.uniform(jax.random.fold_in(jax.random.fold_in(own_key, 6), axis_at), (blocks,), jnp.float32, least / len(cuts), high / len(cuts))
        return jnp.repeat(jnp.exp(heights), shape[axis_at] // blocks).reshape((-1,) + (1,) * (len(shape) - axis_at - 1))

    level = one(*cuts[0])
    for cut in cuts[1:]:
        level = level * one(*cut)
    return level


def scatter_about(key, dims, scale, most, cuts=(), held_as=jnp.bfloat16):
    drawn = jax.random.normal(key, dims, jnp.float32) * scale
    if len(cuts) > 0:
        drawn = steps_of(key, dims, cuts, -0.22, 0.18) * drawn
    return jnp.clip(drawn, min=-most, max=most).astype(held_as)


def setup_inputs(seed: int = 0) -> dict:
    key_of = jax.random.split(jax.random.key(seed), 3)
    return {
        "series": scatter_about(key_of[0], (CH, NSUB), 1.0, 6.0, ((1, 128),), jnp.float32),
        "tail": scatter_about(key_of[1], (CH, M - 1), 1.0, 6.0, (), jnp.float32),
    }


epsilon = 1e-06

def normalize(samples, row_count, sub_length):
    window_index = jnp.arange(row_count, dtype=jnp.int32)[:, None] + jnp.arange(sub_length, dtype=jnp.int32)[None, :]
    windows = samples[window_index]
    average = lax.optimization_barrier(jnp.mean(windows, axis=1, keepdims=True))
    deviation = windows - average
    variance = lax.optimization_barrier(jnp.mean(deviation * deviation, axis=1, keepdims=True))
    return (deviation * lax.rsqrt(variance + epsilon)).astype(jnp.bfloat16)

def single_series(series_row, tail_row):
    devices = N_BAND * N_COL
    padded = jnp.concatenate([series_row, tail_row, jnp.zeros((KD * TB,), series_row.dtype)])
    offsets = jnp.arange(TB, dtype=jnp.int32)

    def visit(position, best_corr):
        position = jnp.asarray(position).astype(jnp.int32)
        start = (position * TB).astype(jnp.int32)
        own_rows = normalize(lax.dynamic_slice_in_dim(padded, start, TB + M - 1), TB, M).astype(jnp.float32)
        for offset in range(KD):
            other = normalize(lax.dynamic_slice_in_dim(padded, start + offset * TB, TB + M - 1), TB, M).astype(jnp.float32)
            scores = jnp.dot(own_rows, other.T, precision=lax.Precision.HIGHEST, preferred_element_type=jnp.float32) / M
            lag_grid = offset * TB + offsets[None, :] - offsets[:, None]
            valid = (jnp.abs(lag_grid) >= EXCL) & (position + offset < devices)
            scores = jnp.where(valid, scores, -4.0)
            row_best = lax.optimization_barrier(jnp.max(scores, axis=1))
            col_best = lax.optimization_barrier(jnp.max(scores, axis=0))
            current = lax.dynamic_slice_in_dim(best_corr, start, TB)
            best_corr = lax.dynamic_update_slice_in_dim(best_corr, jnp.maximum(current, row_best), start, 0)
            target = (jnp.minimum(position + offset, devices - 1) * TB).astype(jnp.int32)
            current = lax.dynamic_slice_in_dim(best_corr, target, TB)
            best_corr = lax.dynamic_update_slice_in_dim(best_corr, jnp.maximum(current, col_best), target, 0)
        return best_corr
    best_corr = lax.fori_loop(0, devices, visit, jnp.full((NSUB,), -4.0, series_row.dtype))
    return jnp.sqrt(2.0 * M * (1.0 - best_corr))

def reference(series, tail):
    return lax.map(lambda pair: single_series(pair[0], pair[1]), (series, tail))
```

```python
import functools

import jax
import jax.numpy as jnp
from jax import lax
from jax.experimental import pallas as pl
from jax.experimental.pallas import tpu as pltpu
from jax.sharding import PartitionSpec as P

AXES = ("band", "col")
KD = 4
EPSILON = 1e-06
ROW = 4
BLOCK = 256
LANES = 128
HALO = KD - 1
SPAN = 2 * HALO + 1


def permute(block, target, count):
    return lax.ppermute(block, AXES, [(i, target(i) % count) for i in range(count)])


def shifted(block, by):
    return pltpu.roll(block, block.shape[1] - by, 1)


def kernel(row_ref, after_ref, before_ref, tail_ref, out_ref, line, wave, mean, scale, z_ref, best_ref):
    channels = out_ref.shape[0]
    place = lax.axis_index("band") * lax.axis_size("col") + lax.axis_index("col")
    count = lax.axis_size("band") * lax.axis_size("col")
    here = lax.rem(place, ROW)

    for piece in range(ROW):
        at = (here ^ piece) * BLOCK
        source = slice(piece * BLOCK, (piece + 1) * BLOCK)
        for turn, ref in enumerate((before_ref, row_ref, after_ref)):
            target = pl.multiple_of(at + turn * ROW * BLOCK, BLOCK)
            line[:, pl.ds(target, BLOCK)] = ref[:, source]

    @pl.when(place + ROW >= count)
    def _():
        line[:, 2 * ROW * BLOCK : 2 * ROW * BLOCK + BLOCK] = tail_ref[...]

    start = pl.multiple_of((here + ROW - HALO) * BLOCK, BLOCK)
    x = line[:, pl.ds(start, (SPAN + 1) * BLOCK)]
    for l in range((SPAN + 1) * 2):
        wave[l] = x[:, l * LANES : (l + 1) * LANES]

    average, spread = x, jnp.zeros_like(x)
    width = 1
    while width < BLOCK:
        other = shifted(average, width)
        gap = other - average
        spread = spread + shifted(spread, width) + gap * gap * (0.5 * width)
        average = average + 0.5 * gap
        width *= 2
    spread = lax.rsqrt(spread * (1.0 / BLOCK) + EPSILON)
    for l in range(SPAN * 2):
        mean[l] = average[:, l * LANES : (l + 1) * LANES]
        scale[l] = spread[:, l * LANES : (l + 1) * LANES]

    low = lax.broadcasted_iota(jnp.int32, (LANES, LANES), 1)
    low = low <= lax.broadcasted_iota(jnp.int32, (LANES, LANES), 0)
    lag = lax.broadcasted_iota(jnp.int32, (BLOCK, BLOCK), 1)
    lag = lag - lax.broadcasted_iota(jnp.int32, (BLOCK, BLOCK), 0)

    def line_of(ref, c, l):
        row = ref[l, pl.ds(c, 8, stride=0), :]
        return jnp.broadcast_to(row[None], (LANES // 8, 8, LANES)).reshape(LANES, LANES)

    def turned(c, l):
        return pltpu.roll(line_of(wave, c, l), 1, 1, stride=1, stride_axis=0)

    def channel(c, carry):
        first = turned(c, 0)
        second = turned(c, 1)
        near = jnp.where(low, first, second)
        for l in range(SPAN * 2):
            third = turned(c, l + 2)
            far = jnp.where(low, second, third)
            at = slice(l * LANES, (l + 1) * LANES)
            a = line_of(mean, c, l)
            r = line_of(scale, c, l)
            z_ref[:LANES, at] = ((near - a) * r).astype(jnp.bfloat16)
            z_ref[LANES:, at] = ((far - a) * r).astype(jnp.bfloat16)
            near, second = far, third
        own = z_ref[:, HALO * BLOCK : (HALO + 1) * BLOCK].T
        best = jnp.full((BLOCK, LANES), -4.0, jnp.float32)
        for b in range(SPAN):
            score = jnp.dot(own, z_ref[:, b * BLOCK : (b + 1) * BLOCK], preferred_element_type=jnp.float32) * (1.0 / BLOCK)
            offset = b - HALO
            if abs(offset) <= 1:
                score = jnp.where(jnp.abs(lag + offset * BLOCK) >= BLOCK // 4, score, -4.0)
            top = jnp.maximum(score[:, :LANES], score[:, LANES:])
            if offset:
                valid = (place + offset >= 0) & (place + offset < count)
                top = jnp.where(valid, top, -4.0)
            best = jnp.maximum(best, top)
        best_ref[pl.ds(c, 1), :] = jnp.max(best.T, axis=0, keepdims=True)
        return carry

    lax.fori_loop(0, channels, channel, 0)
    out_ref[...] = jnp.sqrt(2.0 * BLOCK * (1.0 - best_ref[...]))


def shards(series, tail):
    channels = series.shape[0]
    count = lax.axis_size(AXES)
    tail = jnp.pad(tail, ((0, 0), (0, 1)))
    pair = jnp.concatenate([series, permute(series, lambda i: i ^ 1, count)], axis=1)
    row = jnp.concatenate([pair, permute(pair, lambda i: i ^ 2, count)], axis=1)
    after = permute(row, lambda i: i - ROW, count)
    before = permute(row, lambda i: i + ROW, count)
    vmem = pl.BlockSpec(memory_space=pltpu.VMEM)
    return pl.pallas_call(
        kernel,
        out_shape=jax.ShapeDtypeStruct((channels, BLOCK), jnp.float32),
        in_specs=[vmem] * 4,
        out_specs=vmem,
        scratch_shapes=[
            pltpu.VMEM((channels, 3 * ROW * BLOCK), jnp.float32),
            pltpu.VMEM(((SPAN + 1) * 2, channels, LANES), jnp.float32),
            pltpu.VMEM((SPAN * 2, channels, LANES), jnp.float32),
            pltpu.VMEM((SPAN * 2, channels, LANES), jnp.float32),
            pltpu.VMEM((BLOCK, SPAN * BLOCK), jnp.bfloat16),
            pltpu.VMEM((channels, BLOCK), jnp.float32),
        ],
    )(row, after, before, tail)


def solution(mesh):
    return jax.shard_map(
        shards,
        mesh=mesh,
        in_specs=(P(None, AXES), P()),
        out_specs=P(None, AXES),
        check_vma=False,
    )
```

```python
import functools

import jax
import jax.numpy as jnp
from jax import lax
from jax.experimental import pallas as pl
from jax.experimental.pallas import tpu as pltpu
from jax.sharding import PartitionSpec as P

AXES = ("band", "col")
KD = 4
EPSILON = 1e-06
ROW = 4
BLOCK = 256
LANES = 128
HALO = KD - 1
SPAN = 2 * HALO + 1
UNROLL = 2
CHUNK = 32


def permute(block, target, count):
    return lax.ppermute(block, AXES, [(i, target(i) % count) for i in range(count)])


def kernel(row_ref, after_ref, before_ref, tail_ref, out_ref, line, wave, mean, scale, best_ref, *slots):
    channels = out_ref.shape[0]
    place = lax.axis_index("band") * lax.axis_size("col") + lax.axis_index("col")
    count = lax.axis_size("band") * lax.axis_size("col")
    here = lax.rem(place, ROW)

    for piece in range(ROW):
        at = (here ^ piece) * BLOCK
        source = slice(piece * BLOCK, (piece + 1) * BLOCK)
        for turn, ref in enumerate((before_ref, row_ref, after_ref)):
            target = pl.multiple_of(at + turn * ROW * BLOCK, BLOCK)
            line[:, pl.ds(target, BLOCK)] = ref[:, source]

    @pl.when(place + ROW >= count)
    def _():
        line[:, 2 * ROW * BLOCK : 2 * ROW * BLOCK + BLOCK - 1] = tail_ref[...]

    start = pl.multiple_of((here + ROW - HALO) * BLOCK, BLOCK)
    blocks = (SPAN + 1) * 2
    total = [line[:, pl.ds(pl.multiple_of(start + l * LANES, LANES), LANES)] for l in range(blocks)]
    for l in range(blocks):
        wave[l] = total[l]

    column = lax.broadcasted_iota(jnp.int32, (channels, LANES), 1)

    def shifted(values, by):
        if by == LANES:
            return values[1:] + values[-1:]
        turned = [pltpu.roll(v, LANES - by, 1) for v in values]
        inside = column < LANES - by
        return [jnp.where(inside, t, u) for t, u in zip(turned, turned[1:] + turned[-1:])]

    spread = None
    width = 1
    while width < BLOCK:
        other = shifted(total, width)
        gap = [o - t for o, t in zip(other, total)]
        gap = [g * g * (0.5 / width) for g in gap]
        if spread is None:
            spread = gap
        else:
            spread = [a + b + g for a, b, g in zip(spread, shifted(spread, width), gap)]
        total = [t + o for t, o in zip(total, other)]
        width *= 2
    for l in range(SPAN * 2):
        mean[l] = total[l] * (1.0 / BLOCK)
        scale[l] = lax.rsqrt(spread[l] * (1.0 / BLOCK) + EPSILON)

    behind = lax.broadcasted_iota(jnp.int32, (CHUNK, LANES), 1) - lax.broadcasted_iota(jnp.int32, (CHUNK, LANES), 0)

    def spanned(ref, c, l):
        row = ref[l, pl.ds(c, 8, stride=0), :]
        return jnp.broadcast_to(row[None], (CHUNK // 8, 8, LANES)).reshape(CHUNK, LANES)

    def windows(c, z_ref, own_ref, top_ref):
        for k in range(0, LANES, CHUNK):
            low = behind <= k

            def turned(l):
                return pltpu.roll(spanned(wave, c, l), k + 1, 1, stride=1, stride_axis=0)

            first, second = turned(0), turned(1)
            left = jnp.where(low, first, second)
            for l in range(SPAN * 2):
                third = turned(l + 2)
                right = jnp.where(low, second, third)
                a = spanned(mean, c, l)
                r = spanned(scale, c, l)
                z_ref[l, k : k + CHUNK] = ((left - a) * r).astype(jnp.bfloat16)
                z_ref[l, LANES + k : LANES + k + CHUNK] = ((right - a) * r).astype(jnp.bfloat16)
                left, second = right, third
            yield
        for l in range(2):
            own_ref[l] = z_ref[2 * HALO + l].T
        yield

    edge = BLOCK // 4

    def keep(score, offset):
        lag = lax.broadcasted_iota(jnp.int32, score.shape, 1) - lax.broadcasted_iota(jnp.int32, score.shape, 0)
        return jnp.where(jnp.abs(lag + offset) >= edge, score, -4.0 * BLOCK)

    def source(b):
        exists = (place + b - HALO >= 0) & (place + b - HALO < count)
        return jnp.where(exists, b, HALO + 2 if b < HALO else HALO - 2)

    sources = [HALO if b == HALO else source(b) for b in range(SPAN)]

    def tile(b, z_ref, own_ref, top_ref):
        at = 2 * sources[b]
        z = jnp.concatenate([z_ref[at], z_ref[at + 1]], axis=1)
        offset = b - HALO
        own = jnp.concatenate([own_ref[0], own_ref[1]], axis=0)
        score = jnp.dot(own, z, preferred_element_type=jnp.float32)
        left, rest = score[:, :LANES], score[:, LANES:]
        if offset == 0:
            left = jnp.concatenate([keep(left[: BLOCK - edge], 0), left[BLOCK - edge :]], axis=0)
            rest = jnp.concatenate([rest[:edge], keep(rest[edge:], LANES - edge)], axis=0)
        if offset == 1:
            left = jnp.concatenate([left[: BLOCK - edge], keep(left[BLOCK - edge :], edge)], axis=0)
        if offset == -1:
            rest = jnp.concatenate([keep(rest[:edge], LANES - BLOCK), rest[edge:]], axis=0)
        top = jnp.maximum(left, rest)
        top_ref[...] = jnp.maximum(top_ref[...], top) if b else top

    def finish(c, z_ref, own_ref, top_ref):
        best_ref[pl.ds(c, 1), :] = jnp.max(top_ref[...].T, axis=0, keepdims=True)

    first, second = slots[:3], slots[3:]

    def step(c, now, later):
        ahead = windows(jnp.minimum(c + 1, channels - 1), *later)
        finish(jnp.maximum(c - 1, 0), *later)
        parts = LANES // CHUNK + 1
        for b in range(SPAN):
            for _ in range(parts * b // (SPAN - 1), parts * (b + 1) // (SPAN - 1)):
                next(ahead, None)
            tile(b, *now)

    def several(k, carry):
        for u in range(UNROLL):
            now, later = (second, first) if u % 2 else (first, second)
            step(k * UNROLL + u, now, later)
        return carry

    for _ in windows(0, *first):
        pass
    lax.fori_loop(0, channels // UNROLL, several, 0)
    finish(channels - 1, *second)
    out_ref[...] = jnp.sqrt(2.0 * BLOCK - 2.0 * best_ref[...])


def shards(series, tail):
    channels = series.shape[0]
    count = lax.axis_size(AXES)
    pair = jnp.concatenate([series, permute(series, lambda i: i ^ 1, count)], axis=1)
    row = jnp.concatenate([pair, permute(pair, lambda i: i ^ 2, count)], axis=1)
    after = permute(row, lambda i: i - ROW, count)
    before = permute(row, lambda i: i + ROW, count)
    vmem = pl.BlockSpec(memory_space=pltpu.VMEM)
    return pl.pallas_call(
        kernel,
        out_shape=jax.ShapeDtypeStruct((channels, BLOCK), jnp.float32),
        in_specs=[vmem] * 4,
        out_specs=vmem,
        scratch_shapes=[
            pltpu.VMEM((channels, 3 * ROW * BLOCK), jnp.float32),
            pltpu.VMEM(((SPAN + 1) * 2, channels, LANES), jnp.float32),
            pltpu.VMEM((SPAN * 2, channels, LANES), jnp.float32),
            pltpu.VMEM((SPAN * 2, channels, LANES), jnp.float32),
            pltpu.VMEM((channels, BLOCK), jnp.float32),
        ]
        + [
            pltpu.VMEM((SPAN * 2, BLOCK, LANES), jnp.bfloat16),
            pltpu.VMEM((2, LANES, BLOCK), jnp.bfloat16),
            pltpu.VMEM((BLOCK, LANES), jnp.float32),
        ]
        * 2,
        compiler_params=pltpu.CompilerParams(vmem_limit_bytes=8 << 20),
    )(row, after, before, tail)


def solution(mesh):
    return jax.shard_map(
        shards,
        mesh=mesh,
        in_specs=(P(None, AXES), P()),
        out_specs=P(None, AXES),
        check_vma=False,
    )
```

```python
import jax
import jax.numpy as jnp
from jax import lax
from jax.experimental import pallas as pl
from jax.experimental.pallas import tpu as pltpu
from jax.sharding import PartitionSpec as P


AXES = ("band", "col")
KD = 4
EPSILON = 1e-06
ROW = 4
PAIR = ROW // 2
BLOCK = 256
LANES = 128
HALO = KD - 1
SPAN = 2 * HALO + 1
UNROLL = 2
CHUNK = 32


def permute(block, target, count):
    return lax.ppermute(block, AXES, [(i, target(i) % count) for i in range(count)])


def kernel(pair_ref, across_ref, first_ref, second_ref, third_ref, tail_ref, out_ref, line, wave, mean, scale, best_ref, *slots):
    channels = out_ref.shape[0]
    place = lax.axis_index("band") * lax.axis_size("col") + lax.axis_index("col")
    count = lax.axis_size("band") * lax.axis_size("col")
    here = lax.rem(place, ROW)

    late = here // PAIR
    for ref, other, row in ((pair_ref, 0, 1), (across_ref, PAIR, 1), (first_ref, 0, 2 - 2 * late), (second_ref, 0, 2 * late), (third_ref, PAIR, 2 * late)):
        for piece in range(PAIR):
            target = pl.multiple_of(((here ^ (other + piece)) + ROW * row) * BLOCK, BLOCK)
            line[:, pl.ds(target, BLOCK)] = ref[:, piece * BLOCK : (piece + 1) * BLOCK]

    @pl.when(place + ROW >= count)
    def _():
        line[:, 2 * ROW * BLOCK : 2 * ROW * BLOCK + BLOCK - 1] = tail_ref[...]

    start = pl.multiple_of((here + ROW - HALO) * BLOCK, BLOCK)
    blocks = (SPAN + 1) * 2
    total = [line[:, pl.ds(pl.multiple_of(start + l * LANES, LANES), LANES)] for l in range(blocks)]
    for l in range(blocks):
        wave[l] = total[l]

    column = lax.broadcasted_iota(jnp.int32, (channels, LANES), 1)

    def shifted(values, by):
        if by == LANES:
            return values[1:] + values[-1:]
        turned = [pltpu.roll(v, LANES - by, 1) for v in values]
        inside = column < LANES - by
        return [jnp.where(inside, t, u) for t, u in zip(turned, turned[1:] + turned[-1:])]

    spread = None
    width = 1
    while width < BLOCK:
        other = shifted(total, width)
        gap = [o - t for o, t in zip(other, total)]
        gap = [g * g * (0.5 / width) for g in gap]
        if spread is None:
            spread = gap
        else:
            spread = [a + b + g for a, b, g in zip(spread, shifted(spread, width), gap)]
        total = [t + o for t, o in zip(total, other)]
        width *= 2
    for l in range(SPAN * 2):
        mean[l] = total[l] * (1.0 / BLOCK)
        scale[l] = lax.rsqrt(spread[l] * (1.0 / BLOCK) + EPSILON)

    behind = lax.broadcasted_iota(jnp.int32, (CHUNK, LANES), 1) - lax.broadcasted_iota(jnp.int32, (CHUNK, LANES), 0)

    behind_own = lax.broadcasted_iota(jnp.int32, (LANES, LANES), 1) - lax.broadcasted_iota(jnp.int32, (LANES, LANES), 0)

    def spanned(ref, c, l):
        row = ref[l, pl.ds(c, 8, stride=0), :]
        return jnp.broadcast_to(row[None], (CHUNK // 8, 8, LANES)).reshape(CHUNK, LANES)

    def windows(c, z_ref, own_ref, top_ref):
        for k in range(0, LANES, CHUNK):
            low = behind <= k

            def turned(l):
                return pltpu.roll(spanned(wave, c, l), k + 1, 1, stride=1, stride_axis=0)

            first, second = turned(0), turned(1)
            left = jnp.where(low, first, second)
            for l in range(SPAN * 2):
                third = turned(l + 2)
                right = jnp.where(low, second, third)
                a = spanned(mean, c, l)
                r = spanned(scale, c, l)
                z_ref[l, k : k + CHUNK] = ((left - a) * r).astype(jnp.bfloat16)
                z_ref[l, LANES + k : LANES + k + CHUNK] = ((right - a) * r).astype(jnp.bfloat16)
                left, second = right, third
            yield
        for l in range(2):
            turn = jnp.where(behind_own == 0, 1.0, 0.0).astype(jnp.bfloat16)
            own_ref[l] = lax.dot_general(turn, z_ref[2 * HALO + l], (((1,), (1,)), ((), ())), preferred_element_type=jnp.float32).astype(jnp.bfloat16)
        yield

    edge = BLOCK // 4

    def keep(score, offset):
        lag = lax.broadcasted_iota(jnp.int32, score.shape, 1) - lax.broadcasted_iota(jnp.int32, score.shape, 0)
        return jnp.where(jnp.abs(lag + offset) >= edge, score, -4.0 * BLOCK)

    def source(b):
        exists = (place + b - HALO >= 0) & (place + b - HALO < count)
        return jnp.where(exists, b, HALO + 2 if b < HALO else HALO - 2)

    sources = [HALO if b == HALO else source(b) for b in range(SPAN)]

    def tile(b, z_ref, own_ref, top_ref):
        at = 2 * sources[b]
        z = jnp.concatenate([z_ref[at], z_ref[at + 1]], axis=1)
        offset = b - HALO
        own = jnp.concatenate([own_ref[0], own_ref[1]], axis=0)
        score = jnp.dot(own, z, preferred_element_type=jnp.float32)
        left, rest = score[:, :LANES], score[:, LANES:]
        if offset == 0:
            left = jnp.concatenate([keep(left[: BLOCK - edge], 0), left[BLOCK - edge :]], axis=0)
            rest = jnp.concatenate([rest[:edge], keep(rest[edge:], LANES - edge)], axis=0)
        if offset == 1:
            left = jnp.concatenate([left[: BLOCK - edge], keep(left[BLOCK - edge :], edge)], axis=0)
        if offset == -1:
            rest = jnp.concatenate([keep(rest[:edge], LANES - BLOCK), rest[edge:]], axis=0)
        top = jnp.maximum(left, rest)
        top_ref[...] = jnp.maximum(top_ref[...], top) if b else top

    def finish(c, z_ref, own_ref, top_ref):
        column = lax.broadcasted_iota(jnp.int32, (BLOCK, LANES), 1)
        best_ref[...] = jnp.where(column == c, jnp.max(top_ref[...], axis=1, keepdims=True), best_ref[...])

    first, second = slots[:3], slots[3:]

    def step(c, now, later):
        ahead = windows(jnp.minimum(c + 1, channels - 1), *later)
        parts = LANES // CHUNK + 1
        for b in range(SPAN):
            for _ in range(parts * b // (SPAN - 1), parts * (b + 1) // (SPAN - 1)):
                next(ahead, None)
            tile(b, *now)
            if b == 3:
                finish(jnp.maximum(c - 1, 0), *later)

    def several(k, carry):
        for u in range(UNROLL):
            now, later = (second, first) if u % 2 else (first, second)
            step(k * UNROLL + u, now, later)
        return carry

    for _ in windows(0, *first):
        pass
    lax.fori_loop(0, channels // UNROLL, several, 0)
    finish(channels - 1, *second)
    out_ref[...] = jnp.sqrt(2.0 * BLOCK - 2.0 * best_ref[...].T[:channels])


def shards(series, tail):
    channels = series.shape[0]
    count = lax.axis_size(AXES)
    forward = lambda i: i - ROW if i % ROW < PAIR else i + ROW
    backward = lambda i: i + ROW if i % ROW < PAIR else i - ROW
    pair = jnp.concatenate([series, permute(series, lambda i: i ^ 1, count)], axis=1)
    first = permute(pair, forward, count)
    across = permute(pair, lambda i: i ^ PAIR, count)
    second = permute(pair, backward, count)
    third = permute(first, lambda i: i ^ PAIR, count)
    vmem = pl.BlockSpec(memory_space=pltpu.VMEM)
    return pl.pallas_call(
        kernel,
        out_shape=jax.ShapeDtypeStruct((channels, BLOCK), jnp.float32),
        in_specs=[vmem] * 6,
        out_specs=vmem,
        scratch_shapes=[
            pltpu.VMEM((channels, 3 * ROW * BLOCK), jnp.float32),
            pltpu.VMEM(((SPAN + 1) * 2, channels, LANES), jnp.float32),
            pltpu.VMEM((SPAN * 2, channels, LANES), jnp.float32),
            pltpu.VMEM((SPAN * 2, channels, LANES), jnp.float32),
            pltpu.VMEM((BLOCK, LANES), jnp.float32),
        ]
        + [
            pltpu.VMEM((SPAN * 2, BLOCK, LANES), jnp.bfloat16),
            pltpu.VMEM((2, LANES, BLOCK), jnp.bfloat16),
            pltpu.VMEM((BLOCK, LANES), jnp.float32),
        ]
        * 2,
        compiler_params=pltpu.CompilerParams(vmem_limit_bytes=8 << 20),
    )(pair, across, first, second, third, tail)


def solution(mesh):
    return jax.shard_map(
        shards,
        mesh=mesh,
        in_specs=(P(None, AXES), P()),
        out_specs=P(None, AXES),
        check_vma=False,
    )
```

```python
import jax
import jax.numpy as jnp
from jax import lax
from jax.experimental import pallas as pl
from jax.experimental.pallas import tpu as pltpu
from jax.sharding import PartitionSpec as P


AXES = ("band", "col")
KD = 4
EPSILON = 1e-06
ROW = 4
PAIR = ROW // 2
BLOCK = 256
LANES = 128
HALO = KD - 1
SPAN = 2 * HALO + 1
UNROLL = 4
CHUNK = 32


def permute(block, target, count):
    return lax.ppermute(block, AXES, [(i, target(i) % count) for i in range(count)])


def kernel(pair_ref, across_ref, first_ref, second_ref, third_ref, tail_ref, out_ref, line, wave, mean, scale, best_ref, most_ref, *slots):
    channels = out_ref.shape[0]
    place = lax.axis_index("band") * lax.axis_size("col") + lax.axis_index("col")
    count = lax.axis_size("band") * lax.axis_size("col")
    here = lax.rem(place, ROW)

    late = here // PAIR
    for ref, other, row in ((pair_ref, 0, 1), (across_ref, PAIR, 1), (first_ref, 0, 2 - 2 * late), (second_ref, 0, 2 * late), (third_ref, PAIR, 2 * late)):
        for piece in range(PAIR):
            target = pl.multiple_of(((here ^ (other + piece)) + ROW * row) * BLOCK, BLOCK)
            line[:, pl.ds(target, BLOCK)] = ref[:, piece * BLOCK : (piece + 1) * BLOCK]

    @pl.when(place + ROW >= count)
    def _():
        line[:, 2 * ROW * BLOCK : 2 * ROW * BLOCK + BLOCK - 1] = tail_ref[...]

    start = pl.multiple_of((here + ROW - HALO) * BLOCK, BLOCK)
    blocks = (SPAN + 1) * 2
    total = [line[:, pl.ds(pl.multiple_of(start + l * LANES, LANES), LANES)] for l in range(blocks)]
    for l in range(blocks):
        wave[l] = total[l]

    column = lax.broadcasted_iota(jnp.int32, (channels, LANES), 1)

    def shifted(values, by):
        if by == LANES:
            return values[1:] + values[-1:]
        turned = [pltpu.roll(v, LANES - by, 1) for v in values]
        inside = column < LANES - by
        return [jnp.where(inside, t, u) for t, u in zip(turned, turned[1:] + turned[-1:])]

    spread = None
    width = 1
    while width < BLOCK:
        other = shifted(total, width)
        gap = [o - t for o, t in zip(other, total)]
        gap = [g * g * (0.5 / width) for g in gap]
        if spread is None:
            spread = gap
        else:
            spread = [a + b + g for a, b, g in zip(spread, shifted(spread, width), gap)]
        total = [t + o for t, o in zip(total, other)]
        width *= 2
    for l in range(SPAN * 2):
        mean[l] = total[l] * (1.0 / BLOCK)
        scale[l] = lax.rsqrt(spread[l] * (1.0 / BLOCK) + EPSILON)

    behind = lax.broadcasted_iota(jnp.int32, (CHUNK, LANES), 1) - lax.broadcasted_iota(jnp.int32, (CHUNK, LANES), 0)

    behind_own = lax.broadcasted_iota(jnp.int32, (LANES, LANES), 1) - lax.broadcasted_iota(jnp.int32, (LANES, LANES), 0)

    def spanned(ref, c, l):
        row = ref[l, pl.ds(c, 8, stride=0), :]
        return jnp.broadcast_to(row[None], (CHUNK // 8, 8, LANES)).reshape(CHUNK, LANES)

    def windows(c, z_ref, own_ref, top_ref):
        for k in range(0, LANES, CHUNK):
            low = behind <= k

            def turned(l):
                return pltpu.roll(spanned(wave, c, l), k + 1, 1, stride=1, stride_axis=0)

            first, second = turned(0), turned(1)
            left = jnp.where(low, first, second)
            for l in range(SPAN * 2):
                third = turned(l + 2)
                right = jnp.where(low, second, third)
                a = spanned(mean, c, l)
                r = spanned(scale, c, l)
                z_ref[l, k : k + CHUNK] = ((left - a) * r).astype(jnp.bfloat16)
                z_ref[l, LANES + k : LANES + k + CHUNK] = ((right - a) * r).astype(jnp.bfloat16)
                left, second = right, third
            yield
        for l in range(2):
            turn = jnp.where(behind_own == 0, 1.0, 0.0).astype(jnp.bfloat16)
            own_ref[l] = lax.dot_general(turn, z_ref[2 * HALO + l], (((1,), (1,)), ((), ())), preferred_element_type=jnp.float32).astype(jnp.bfloat16)
        yield

    edge = BLOCK // 4

    lag = lax.broadcasted_iota(jnp.int32, (BLOCK, BLOCK), 1) - lax.broadcasted_iota(jnp.int32, (BLOCK, BLOCK), 0)
    most_ref[...] = jnp.where(jnp.abs(lag) >= edge, 1e30, -4.0 * BLOCK)

    def keep(score, row, column):
        rows, columns = score.shape
        return jnp.minimum(score, most_ref[row : row + rows, column : column + columns])

    def source(b):
        exists = (place + b - HALO >= 0) & (place + b - HALO < count)
        return jnp.where(exists, b, HALO + 2 if b < HALO else HALO - 2)

    sources = [HALO if b == HALO else source(b) for b in range(SPAN)]

    def tile(b, fresh, z_ref, own_ref, top_ref):
        at = 2 * sources[b]
        z = jnp.concatenate([z_ref[at], z_ref[at + 1]], axis=1)
        offset = b - HALO
        own = jnp.concatenate([own_ref[0], own_ref[1]], axis=0)
        score = jnp.dot(own, z, preferred_element_type=jnp.float32)
        left, rest = score[:, :LANES], score[:, LANES:]
        if offset == 0:
            left = jnp.concatenate([keep(left[: BLOCK - edge], 0, 0), left[BLOCK - edge :]], axis=0)
            rest = jnp.concatenate([rest[:edge], keep(rest[edge:], edge, LANES)], axis=0)
        if offset == 1:
            left = jnp.concatenate([left[: BLOCK - edge], keep(left[BLOCK - edge :], edge, LANES)], axis=0)
        if offset == -1:
            rest = jnp.concatenate([keep(rest[:edge], LANES, 0), rest[edge:]], axis=0)
        top = jnp.maximum(left, rest)
        top_ref[...] = top if fresh else jnp.maximum(top_ref[...], top)

    def finish(c, z_ref, own_ref, top_ref):
        column = lax.broadcasted_iota(jnp.int32, (BLOCK, LANES), 1)
        best_ref[...] = jnp.where(column == c, jnp.max(top_ref[...], axis=1, keepdims=True), best_ref[...])

    first, second = slots[:3], slots[3:]

    def step(c, now, later):
        ahead = windows(jnp.minimum(c + 1, channels - 1), *later)
        for n, b in enumerate((0, 1, 2, 4, 5, 6, 3)):
            for _ in range((2, 3, 4, 5, 6).count(n)):
                next(ahead)
            tile(b, n == 0, *now)
            if n == 3:
                finish(jnp.maximum(c - 1, 0), *later)

    def several(k, carry):
        for u in range(UNROLL):
            now, later = (second, first) if u % 2 else (first, second)
            step(k * UNROLL + u, now, later)
        return carry

    for _ in windows(0, *first):
        pass
    lax.fori_loop(0, channels // UNROLL, several, 0)
    finish(channels - 1, *second)
    out_ref[...] = jnp.sqrt(2.0 * BLOCK - 2.0 * best_ref[...].T[:channels])


def shards(series, tail):
    channels = series.shape[0]
    count = lax.axis_size(AXES)
    forward = lambda i: i - ROW if i % ROW < PAIR else i + ROW
    backward = lambda i: i + ROW if i % ROW < PAIR else i - ROW
    pair = jnp.concatenate([series, permute(series, lambda i: i ^ 1, count)], axis=1)
    first = permute(pair, forward, count)
    across = permute(pair, lambda i: i ^ PAIR, count)
    second = permute(pair, backward, count)
    third = permute(first, lambda i: i ^ PAIR, count)
    vmem = pl.BlockSpec(memory_space=pltpu.VMEM)
    return pl.pallas_call(
        kernel,
        out_shape=jax.ShapeDtypeStruct((channels, BLOCK), jnp.float32),
        in_specs=[vmem] * 6,
        out_specs=vmem,
        scratch_shapes=[
            pltpu.VMEM((channels, 3 * ROW * BLOCK), jnp.float32),
            pltpu.VMEM(((SPAN + 1) * 2, channels, LANES), jnp.float32),
            pltpu.VMEM((SPAN * 2, channels, LANES), jnp.float32),
            pltpu.VMEM((SPAN * 2, channels, LANES), jnp.float32),
            pltpu.VMEM((BLOCK, LANES), jnp.float32),
            pltpu.VMEM((BLOCK, BLOCK), jnp.float32),
        ]
        + [
            pltpu.VMEM((SPAN * 2, BLOCK, LANES), jnp.bfloat16),
            pltpu.VMEM((2, LANES, BLOCK), jnp.bfloat16),
            pltpu.VMEM((BLOCK, LANES), jnp.float32),
        ]
        * 2,
        compiler_params=pltpu.CompilerParams(vmem_limit_bytes=8 << 20),
    )(pair, across, first, second, third, tail)


def solution(mesh):
    return jax.shard_map(
        shards,
        mesh=mesh,
        in_specs=(P(None, AXES), P()),
        out_specs=P(None, AXES),
        check_vma=False,
    )
```
